256 devices in a mesh: row: 8 (over x_hi, y), col: 32 (over x_lo, z, core).
Axes of the slice: x: 4 (x_hi: 2, x_lo: 2; x = x_hi * 2 + x_lo), y: 4, z: 8, core: 2. Of those that a mesh axis runs over, the one named last changes fastest.
Arguments:
- orbitals: bfloat16 [16384, 1024], P('row', 'col'), may hold values from -0.1875 to 0.1875
- kernel: bfloat16 [16384, 16384], P('col', 'row'), may hold values from -6 to 6
- applied: bfloat16 [16384, 512], P('col', 'row'), may hold values from -1.5 to 1.5
- fit: bfloat16 [16384, 65536], P('row', 'col'), may hold values from -0.046875 to 0.046875
Outputs:
- exchange_term: bfloat16 [512, 65536], P('row', 'col')
The draws below stay inside these ranges and needn't reach their ends.
All inputs are finite; a program needn't handle non-finite values.
Results may differ from the reference program's by a relative error of at most 0.0058.
Values may be sent and summed in bfloat16 or wider, within the bound.
No kernel may reach another device: no remote copies, remote signals or barrier semaphores. Data moves between devices by JAX's collectives and lax.ppermute only.
A program may use at most 64 MiB of HBM per device.

```python
import jax
import jax.numpy as jnp
from jax import lax

NORB = 1024
NMU = 16384
NAPP = 512
NG = 65536
N_COL = 32


def shard_levels(own_key, dims, split, low, top_value):
    factor_of = 1.0
    for dim, blocks in split:
        draws = jax.random.uniform(jax.random.fold_in(jax.random.fold_in(own_key, 6), dim), (blocks,), jnp.float32, low / len(split), top_value / len(split))
        factor_of = factor_of * jnp.repeat(jnp.exp(draws), dims[dim] // blocks).reshape((-1,) + (1,) * (len(dims) - 1 - dim))
    return factor_of


def bell_draw(stream_key, shape, spread, bound, split=(), dtype=jnp.bfloat16):
    values = jax.random.normal(stream_key, shape, jnp.float32) * spread
    if len(split) > 0:
        values = shard_levels(stream_key, shape, split, -0.22, 0.18) * values
    return jnp.clip(values, min=-bound, max=bound).astype(dtype)


def setup_inputs(seed: int = 0) -> dict:
    key_of = jax.random.split(jax.random.key(seed), 5)
    return {
        "orbitals": bell_draw(key_of[0], (NMU, NORB), NORB ** -0.5, 0.1875, ((0, 8), (1, 32))),
        "kernel": bell_draw(key_of[1], (NMU, NMU), 1.0, 6.0, ((0, 32), (1, 8))),
        "applied": bell_draw(key_of[2], (NMU, NAPP), 0.25, 1.5, ((0, 32), (1, 8))),
        "fit": bell_draw(key_of[3], (NMU, NG), NMU ** -0.5, 0.046875, ((0, 8), (1, 32))),
    }


def reference(orbitals, kernel, applied, fit):
    blocks = N_COL
    width = NMU // blocks
    orb_blocks = orbitals.reshape(blocks, width, NORB)
    kernel_blocks = kernel.reshape(blocks, width, NMU)
    applied_blocks = applied.reshape(blocks, width, NAPP)

    def accumulate(projected, items):
        orb_part, kernel_part, applied_part = items
        density = jnp.dot(orb_part, orbitals.T, preferred_element_type=jnp.float32)
        weighted = (density * kernel_part.astype(jnp.float32)).astype(jnp.bfloat16)
        return projected + jnp.dot(weighted.T, applied_part, preferred_element_type=jnp.float32), None

    projected, _ = lax.scan(accumulate, jnp.zeros((NMU, NAPP), jnp.float32), (orb_blocks, kernel_blocks, applied_blocks))
    projected_low = projected.astype(jnp.bfloat16)
    result = jnp.dot(projected_low.T, fit, preferred_element_type=jnp.float32)
    return (-result).astype(jnp.bfloat16)
```

```python
import jax
import jax.numpy as jnp
from jax import lax
from jax.sharding import Mesh
from jax.sharding import PartitionSpec as P

BF = jnp.bfloat16
F32 = jnp.float32
ROW = ("xh", "y")
Z = ("zh", "zl")
SIZES = (("xh", 2), ("y", 4), ("xl", 2), ("zh", 4), ("zl", 2), ("core", 2))
NAMES = tuple(name for name, _ in SIZES)
PAIR = ((0, 1), (1, 0))
CHUNKS = 2


def flat(coords):
    index = 0
    for (_, size), value in zip(SIZES, coords):
        index = index * size + value
    return index


def swap_pairs():
    pairs = []
    for a in range(2):
        for b in range(4):
            for c in range(2):
                for d in range(4):
                    for e in range(2):
                        for f in range(2):
                            pairs.append((flat((a, b, c, d, e, f)), flat((c, d, a, b, e, f))))
    return pairs


def dot(a, b):
    return lax.dot_general(a, b, (((0,), (0,)), ((), ())), preferred_element_type=F32)


def swap(x, axis):
    return lax.ppermute(x, axis, PAIR)


def gather(x, axes, count):
    copies = jnp.broadcast_to(x[None], (count,) + x.shape)
    return lax.all_to_all(copies, axes, 0, 0, tiled=False)


def half(x, index, axis):
    size = x.shape[axis] // 2
    return lax.dynamic_slice_in_dim(x, index * size, size, axis)


def total(terms):
    parts = [terms[k].astype(F32) for k in range(terms.shape[0])]
    while len(parts) > 1:
        parts = [a + b for a, b in zip(parts[::2], parts[1::2])]
    return parts[0]


def ordered(index, own, other):
    first = jnp.where(index == 0, own, other)
    second = jnp.where(index == 0, other, own)
    return first, second


def per_device(orbitals, kernel, applied, fit):
    core = lax.axis_index("core")
    xl = lax.axis_index("xl")
    zl = lax.axis_index("zl")

    bands = orbitals.T
    with jax.named_scope("mu"):
        mu_own = half(bands, core, 1)
        mu_other = swap(half(bands, 1 - core, 1), "core")
        mu_a = gather(mu_own, Z, 8).reshape(256, 1024)
        mu_b = gather(mu_other, Z, 8).reshape(256, 1024)
        mu_ax = swap(mu_a, "xl")
        mu_bx = swap(mu_b, "xl")
    with jax.named_scope("nu"):
        low, high = ordered(zl, half(bands, zl, 1), swap(half(bands, 1 - zl, 1), "zl"))
        piece = jnp.concatenate([low, high], axis=0)
        piece = lax.ppermute(piece, NAMES, swap_pairs())
        both_a = gather(jnp.concatenate([piece, applied.T], axis=1), ROW, 8)
        both_b = swap(both_a, "core")
        nu_a = both_a[:, :, :1024].reshape(512, 1024)
        nu_b = both_b[:, :, :1024].reshape(512, 1024)
        blocks = jnp.concatenate(ordered(core, both_a[:, :, 1024:], both_b[:, :, 1024:]), axis=2)
    with jax.named_scope("kernel"):
        own = half(kernel, core, 1)
        other = swap(half(kernel, 1 - core, 1), "core")
        weights = jnp.concatenate(ordered(core, own, other), axis=0)
    with jax.named_scope("fit"):
        place = core * 2 + xl
        fits = [
            lax.dynamic_slice_in_dim(fit, jnp.bitwise_xor(place, k) * 512, 512, 0) for k in range(4)
        ]

    with jax.named_scope("density"):
        density = dot(half(nu_a, xl, 0), mu_a)
        density = density + dot(half(nu_b, xl, 0), mu_b)
        density = density + dot(half(nu_a, 1 - xl, 0), mu_ax)
        density = density + dot(half(nu_b, 1 - xl, 0), mu_bx)
        weighted = (density * weights.astype(F32)).astype(BF)
        weighted = lax.optimization_barrier(weighted)

    outs = []
    width = 64 // CHUNKS
    for h in range(CHUNKS):
        with jax.named_scope(f"projected{h}"):
            block = blocks[:, h * width : (h + 1) * width].reshape(8 * width, 1024)
            partial = lax.dot_general(
                weighted, block, (((0,), (1,)), ((), ())), preferred_element_type=F32
            )
            arrived = swap(half(partial, 1 - xl, 0).astype(BF), "xl")
            two = (half(partial, xl, 0) + arrived.astype(F32)).astype(BF)
            terms = lax.all_to_all(two.reshape(8, 64, 8 * width), Z, 0, 0, tiled=False)
            low = total(terms).astype(BF)
            p0 = gather(low, Z, 8).reshape(512, 8 * width)
            p1 = swap(p0, "xl")
            p2 = swap(p0, "core")
            p3 = swap(p1, "core")
        with jax.named_scope(f"exchange{h}"):
            result = dot(p0, fits[0])
            result = result + dot(p1, fits[1])
            result = result + dot(p2, fits[2])
            result = result + dot(p3, fits[3])
            terms = lax.all_to_all(
                (-result).astype(BF).reshape(8, width, 2048), ROW, 0, 0, tiled=False
            )
            outs.append(total(terms).astype(BF))
    return jnp.concatenate(outs, axis=0)


def solution(mesh):
    fine = Mesh(mesh.devices.reshape(tuple(size for _, size in SIZES)), NAMES)
    row, col = ROW, ("xl",) + Z + ("core",)
    return jax.shard_map(
        per_device,
        mesh=fine,
        in_specs=(P(row, col), P(col, row), P(col, row), P(row, col)),
        out_specs=P(row, col),
        check_vma=False,
    )
```

```python
import jax
import jax.numpy as jnp
from jax import lax
from jax.sharding import Mesh
from jax.sharding import PartitionSpec as P


BF = jnp.bfloat16
F32 = jnp.float32
ROW = ("xh", "y")
Z = ("zh", "zl")
SIZES = (("xh", 2), ("y", 4), ("xl", 2), ("zh", 4), ("zl", 2), ("core", 2))
NAMES = tuple(name for name, _ in SIZES)
PAIR = ((0, 1), (1, 0))
MATE = tuple((z, z ^ 1) for z in range(8))
STEPS = (0, 3, 1, 2)
ORDER = (1, 0, 7, 6, 3, 2, 5, 4)
OUTER = tuple((z, (z - 1) % 8 if z % 2 == 0 else (z + 1) % 8) for z in range(8))


def flat(coords):
    index = 0
    for (_, size), value in zip(SIZES, coords):
        index = index * size + value
    return index


def nu_pairs(cross):
    pairs = []
    for xh in range(2):
        for y in range(4):
            for xl in range(2):
                for zh in range(4):
                    for zl in range(2):
                        for core in range(2):
                            away = STEPS[y] if zl == 0 else -STEPS[y]
                            source = (xl, zh, xl ^ xh, (zh + away) % 4, zl ^ cross, core)
                            pairs.append((flat(source), flat((xh, y, xl, zh, zl, core))))
    return pairs


def dot(a, b):
    return lax.dot_general(a, b, (((0,), (0,)), ((), ())), preferred_element_type=F32)


def swap(x, axis):
    return lax.ppermute(x, axis, PAIR)


def gather(x, axes, count):
    copies = jnp.broadcast_to(x[None], (count,) + x.shape)
    return lax.all_to_all(copies, axes, 0, 0, tiled=False)


def ring(x):
    near, far = [x], [x]
    for step in range(1, 5):
        near.append(lax.ppermute(far[step - 1], Z, MATE))
        if step < 4:
            far.append(lax.ppermute(near[step - 1], Z, OUTER))
    return near + far[:0:-1]


def half(x, index, axis):
    size = x.shape[axis] // 2
    return lax.dynamic_slice_in_dim(x, index * size, size, axis)


def total(terms):
    parts = [terms[k].astype(F32) for k in range(terms.shape[0])]
    while len(parts) > 1:
        parts = [a + b for a, b in zip(parts[::2], parts[1::2])]
    return parts[0]


def ordered(index, own, other):
    first = jnp.where(index == 0, own, other)
    second = jnp.where(index == 0, other, own)
    return first, second


def program(orbitals, kernel, applied, fit):
    core = lax.axis_index("core")
    xl = lax.axis_index("xl")
    zl = lax.axis_index("zl")

    bands = orbitals.T
    same = lax.ppermute(half(bands, zl, 1), NAMES, nu_pairs(0))
    cross = lax.ppermute(half(bands, 1 - zl, 1), NAMES, nu_pairs(1))
    piece = jnp.concatenate([cross, same], axis=0)
    both = gather(jnp.concatenate([piece, applied.T], axis=1), ROW, 8)
    nu_a = both[:, :, :1024].reshape(512, 1024)
    nu_b = swap(nu_a, "core")
    own = both[:, :, 1024:].reshape(512, 512)
    other = swap(own, "core")
    blocks = jnp.concatenate(ordered(core, own, other), axis=1)
    mu_own = half(bands, core, 1)
    mu_other = swap(half(bands, 1 - core, 1), "core")
    near = ring(jnp.concatenate([mu_own, mu_other], axis=0))
    away = [None] * 8
    away[0] = swap(near[0], "xl")
    for a, b in ((1, 7), (2, 6), (3, 5)):
        two = swap(jnp.concatenate([near[a], near[b]], axis=0), "xl")
        away[a], away[b] = two[:64], two[64:]
    away[4] = swap(near[4], "xl")
    mu = [
        jnp.concatenate([pieces[n][k * 32 : k * 32 + 32] for n in ORDER], axis=0)
        for pieces in (near, away)
        for k in range(2)
    ]
    own = half(kernel, core, 1)
    other = swap(half(kernel, 1 - core, 1), "core")
    weights = jnp.concatenate(ordered(core, own, other), axis=0)
    place = core * 2 + xl
    fits = [
        lax.dynamic_slice_in_dim(fit, jnp.bitwise_xor(place, k) * 512, 512, 0) for k in range(4)
    ]
    fits = lax.optimization_barrier(fits)

    density = dot(nu_a[:256], mu[0])
    density = density + dot(nu_b[:256], mu[1])
    density = density + dot(nu_a[256:], mu[2])
    density = density + dot(nu_b[256:], mu[3])
    weighted = (density * weights.astype(F32)).astype(BF)
    weighted = lax.optimization_barrier(weighted)

    partial = lax.dot_general(
        weighted, blocks, (((0,), (1,)), ((), ())), preferred_element_type=F32
    )
    arrived = swap(half(partial, 1 - xl, 0).astype(BF), "xl")
    two = (half(partial, xl, 0) + arrived.astype(F32)).astype(BF)
    terms = lax.all_to_all(two.reshape(8, 64, 512), Z, 0, 0, tiled=False)
    low = total(terms).astype(BF)
    p0 = gather(low, Z, 8).reshape(512, 512)
    p1 = swap(p0, "xl")
    p2 = swap(p0, "core")
    p3 = swap(p1, "core")
    result = dot(p0, fits[0])
    result = result + dot(p2, fits[2])
    result = result + dot(p1, fits[1])
    result = result + dot(p3, fits[3])
    terms = lax.all_to_all((-result).astype(BF).reshape(8, 64, 2048), ROW, 0, 0, tiled=False)
    return total(terms).astype(BF)


def solution(mesh):
    fine = Mesh(mesh.devices.reshape(tuple(size for _, size in SIZES)), NAMES)
    row, col = ROW, ("xl",) + Z + ("core",)
    return jax.shard_map(
        program,
        mesh=fine,
        in_specs=(P(row, col), P(col, row), P(col, row), P(row, col)),
        out_specs=P(row, col),
        check_vma=False,
    )
```

```python
import jax
import jax.numpy as jnp
from jax import lax
from jax.sharding import Mesh
from jax.sharding import PartitionSpec as P


BF = jnp.bfloat16
F32 = jnp.float32
ROW = ("xh", "y")
Z = ("zh", "zl")
SIZES = (("xh", 2), ("y", 4), ("xl", 2), ("zh", 4), ("zl", 2), ("core", 2))
NAMES = tuple(name for name, _ in SIZES)
PAIR = ((0, 1), (1, 0))
MATE = tuple((z, z ^ 1) for z in range(8))
STEPS = (0, 3, 1, 2)
ORDER = (1, 0, 7, 6, 3, 2, 5, 4)
OUTER = tuple((z, (z - 1) % 8 if z % 2 == 0 else (z + 1) % 8) for z in range(8))


def flat(coords):
    index = 0
    for (_, size), value in zip(SIZES, coords):
        index = index * size + value
    return index


def nu_pairs():
    pairs = []
    for xh in range(2):
        for y in range(4):
            for xl in range(2):
                for zh in range(4):
                    for zl in range(2):
                        for core in range(2):
                            away = STEPS[y] if zl == 0 else -STEPS[y]
                            source = (xl, zh, xl ^ xh, (zh + away) % 4, zl, core)
                            pairs.append((flat(source), flat((xh, y, xl, zh, zl, core))))
    return pairs


def dot(a, b):
    return lax.dot_general(a, b, (((0,), (0,)), ((), ())), preferred_element_type=F32)


def swap(x, axis):
    return lax.ppermute(x, axis, PAIR)


def gather(x, axes, count):
    copies = jnp.broadcast_to(x[None], (count,) + x.shape)
    return lax.all_to_all(copies, axes, 0, 0, tiled=False)


def ring(x):
    near, far = [x], [x]
    for step in range(1, 5):
        near.append(lax.ppermute(far[step - 1], Z, MATE))
        if step < 4:
            far.append(lax.ppermute(near[step - 1], Z, OUTER))
    return near + far[:0:-1]


def half(x, index, axis):
    size = x.shape[axis] // 2
    return lax.dynamic_slice_in_dim(x, index * size, size, axis)


def total(terms):
    parts = [terms[k].astype(F32) for k in range(terms.shape[0])]
    while len(parts) > 1:
        parts = [a + b for a, b in zip(parts[::2], parts[1::2])]
    return parts[0]


def ordered(index, own, other):
    first = jnp.where(index == 0, own, other)
    second = jnp.where(index == 0, other, own)
    return first, second


def program(orbitals, kernel, applied, fit):
    core = lax.axis_index("core")
    xl = lax.axis_index("xl")
    zl = lax.axis_index("zl")

    bands = orbitals.T
    cross = swap(half(bands, 1 - zl, 1), "zl")
    piece = jnp.concatenate([cross, half(bands, zl, 1)], axis=0)
    piece = lax.ppermute(piece, NAMES, nu_pairs())
    piece = jnp.concatenate([piece, applied.T], axis=1)
    other = swap(piece, "xh")
    both = gather(jnp.stack(ordered(lax.axis_index("xh"), piece, other)), "y", 4)
    nu_a = jnp.transpose(both[:, :, :, :1024], (1, 0, 2, 3)).reshape(512, 1024)
    nu_b = swap(nu_a, "core")
    own = both[:, :, :, 1024:].reshape(512, 512)
    other = swap(own, "core")
    blocks = jnp.concatenate(ordered(core, own, other), axis=1)
    mu_own = half(bands, core, 1)
    mu_other = swap(half(bands, 1 - core, 1), "core")
    near = ring(jnp.concatenate([mu_own, mu_other], axis=0))
    away = [None] * 8
    away[0] = swap(near[0], "xl")
    for a, b in ((1, 7), (2, 6), (3, 5)):
        two = swap(jnp.concatenate([near[a], near[b]], axis=0), "xl")
        away[a], away[b] = two[:64], two[64:]
    away[4] = swap(near[4], "xl")
    mu = [
        jnp.concatenate([pieces[n][k * 32 : k * 32 + 32] for n in ORDER], axis=0)
        for pieces in (near, away)
        for k in range(2)
    ]
    own = half(kernel, core, 1)
    other = swap(half(kernel, 1 - core, 1), "core")
    weights = jnp.concatenate(ordered(core, own, other), axis=0)
    place = core * 2 + xl
    fits = [
        lax.dynamic_slice_in_dim(fit, jnp.bitwise_xor(place, k) * 512, 512, 0) for k in range(4)
    ]
    fits = lax.optimization_barrier(fits)

    density = dot(nu_a[:256], mu[0])
    density = density + dot(nu_b[:256], mu[1])
    density = density + dot(nu_a[256:], mu[2])
    density = density + dot(nu_b[256:], mu[3])
    weighted = (density * weights.astype(F32)).astype(BF)
    weighted = lax.optimization_barrier(weighted)

    partial = lax.dot_general(
        weighted, blocks, (((0,), (1,)), ((), ())), preferred_element_type=F32
    )
    arrived = swap(half(partial, 1 - xl, 0).astype(BF), "xl")
    two = (half(partial, xl, 0) + arrived.astype(F32)).astype(BF)
    terms = lax.all_to_all(two.reshape(8, 64, 512), Z, 0, 0, tiled=False)
    low = total(terms).astype(BF)
    p0 = gather(low, Z, 8).reshape(512, 512)
    p1 = swap(p0, "xl")
    p2 = swap(p0, "core")
    p3 = swap(p1, "core")
    result = dot(p0, fits[0])
    result = result + dot(p2, fits[2])
    result = result + dot(p1, fits[1])
    result = result + dot(p3, fits[3])
    terms = lax.all_to_all((-result).astype(BF).reshape(8, 64, 2048), ("y", "xh"), 0, 0, tiled=False)
    return total(terms).astype(BF)


def solution(mesh):
    fine = Mesh(mesh.devices.reshape(tuple(size for _, size in SIZES)), NAMES)
    row, col = ROW, ("xl",) + Z + ("core",)
    return jax.shard_map(
        program,
        mesh=fine,
        in_specs=(P(row, col), P(col, row), P(col, row), P(row, col)),
        out_specs=P(row, col),
        check_vma=False,
    )
```

```python
import jax
import jax.numpy as jnp
from jax import lax
from jax.experimental import pallas as pl
from jax.experimental.pallas import tpu as pltpu
from jax.sharding import Mesh
from jax.sharding import PartitionSpec as P


BF = jnp.bfloat16
F32 = jnp.float32
ROW = ("xh", "y")
Z = ("zh", "zl")
SIZES = (("xh", 2), ("y", 4), ("xl", 2), ("zh", 4), ("zl", 2), ("core", 2))
NAMES = tuple(name for name, _ in SIZES)
PAIR = ((0, 1), (1, 0))
MATE = tuple((z, z ^ 1) for z in range(8))
STEPS = (0, 3, 1, 2)
ORDER = (1, 0, 7, 6, 3, 2, 5, 4)
OUTER = tuple((z, (z - 1) % 8 if z % 2 == 0 else (z + 1) % 8) for z in range(8))


def flat(coords):
    index = 0
    for (_, size), value in zip(SIZES, coords):
        index = index * size + value
    return index


def nu_pairs():
    pairs = []
    for xh in range(2):
        for y in range(4):
            for xl in range(2):
                for zh in range(4):
                    for zl in range(2):
                        for core in range(2):
                            away = STEPS[y] if zl == 0 else -STEPS[y]
                            source = (xl, zh, xl ^ xh, (zh + away) % 4, zl, core)
                            pairs.append((flat(source), flat((xh, y, xl, zh, zl, core))))
    return pairs


def dot(a, b):
    return lax.dot_general(a, b, (((0,), (0,)), ((), ())), preferred_element_type=F32)


def swap(x, axis):
    return lax.ppermute(x, axis, PAIR)


def gather(x, axes, count):
    copies = jnp.broadcast_to(x[None], (count,) + x.shape)
    return lax.all_to_all(copies, axes, 0, 0, tiled=False)


def ring(x):
    near, far = [x], [x]
    for step in range(1, 5):
        near.append(lax.ppermute(far[step - 1], Z, MATE))
        if step < 4:
            far.append(lax.ppermute(near[step - 1], Z, OUTER))
    return near + far[:0:-1]


def half(x, index, axis):
    size = x.shape[axis] // 2
    return lax.dynamic_slice_in_dim(x, index * size, size, axis)


def total(terms):
    parts = [terms[k].astype(F32) for k in range(terms.shape[0])]
    while len(parts) > 1:
        parts = [a + b for a, b in zip(parts[::2], parts[1::2])]
    return parts[0]


def ordered(index, own, other):
    first = jnp.where(index == 0, own, other)
    second = jnp.where(index == 0, other, own)
    return first, second


def weigh(core, nu_a, nu_b, near, away, own, other):
    def body(core_ref, nu_a_ref, nu_b_ref, *refs):
        near_refs, away_refs = refs[:8], refs[8:13]
        own_ref, other_ref, out_ref, mu_a, mu_b = refs[13:]
        across = {
            0: (away_refs[0], 0),
            1: (away_refs[1], 0),
            7: (away_refs[1], 64),
            2: (away_refs[2], 0),
            6: (away_refs[2], 64),
            3: (away_refs[3], 0),
            5: (away_refs[3], 64),
            4: (away_refs[4], 0),
        }
        for y in range(4):
            for o in range(2):
                n = ORDER[y * 2 + o]
                for x, (ref, start) in enumerate(((near_refs[n], 0), across[n])):
                    row = (y * 2 + x) * 64 + o * 32
                    mu_a[row : row + 32, :] = ref[start : start + 32, :]
                    mu_b[row : row + 32, :] = ref[start + 32 : start + 64, :]

        mine = core_ref[0]

        def tile(t, carry):
            start = pl.multiple_of(t * 256, 256)
            part_a = nu_a_ref[:, :, :, pl.ds(start, 256)].reshape(512, 256)
            part_b = nu_b_ref[:, :, :, pl.ds(start, 256)].reshape(512, 256)
            density = dot(part_a, mu_a[...]) + dot(part_b, mu_b[...])
            row = pl.multiple_of((t % 2) * 256, 256)
            ours = own_ref[pl.ds(row, 256), :]
            theirs = other_ref[pl.ds(row, 256), :]
            factor = jnp.where(t // 2 == mine, ours.astype(F32), theirs.astype(F32))
            out_ref[pl.ds(start, 256), :] = (density * factor).astype(BF)
            return carry

        lax.fori_loop(0, 4, tile, 0)

    vmem = pl.BlockSpec(memory_space=pltpu.VMEM)
    return pl.pallas_call(
        body,
        out_shape=jax.ShapeDtypeStruct((1024, 1024), BF),
        in_specs=[pl.BlockSpec(memory_space=pltpu.SMEM)] + [vmem] * 17,
        out_specs=vmem,
        scratch_shapes=[pltpu.VMEM((512, 1024), BF), pltpu.VMEM((512, 1024), BF)],
        compiler_params=pltpu.CompilerParams(vmem_limit_bytes=32 << 20),
        cost_estimate=pl.CostEstimate(
            flops=2 * 1024**3, bytes_accessed=10 << 20, transcendentals=0
        ),
    )(core.reshape(1), nu_a, nu_b, *near, *away, own, other)


def program(orbitals, kernel, applied, fit):
    core = lax.axis_index("core")
    xl = lax.axis_index("xl")
    zl = lax.axis_index("zl")

    bands = orbitals.T
    cross = swap(half(bands, 1 - zl, 1), "zl")
    piece = jnp.concatenate([cross, half(bands, zl, 1)], axis=0)
    piece = lax.ppermute(piece, NAMES, nu_pairs())
    piece = jnp.concatenate([piece, applied.T], axis=1)
    other = swap(piece, "xh")
    both = gather(jnp.stack(ordered(lax.axis_index("xh"), piece, other)), "y", 4)
    partner = swap(both, "core")
    sides = ordered(core, both[:, :, :, 1024:], partner[:, :, :, 1024:])
    blocks = jnp.concatenate(sides, axis=3).reshape(512, 1024)
    mu_own = half(bands, core, 1)
    mu_other = swap(half(bands, 1 - core, 1), "core")
    near = ring(jnp.concatenate([mu_own, mu_other], axis=0))
    away = []
    for a, b in ((0, 0), (1, 7), (2, 6), (3, 5), (4, 4)):
        piece = near[a] if a == b else jnp.concatenate([near[a], near[b]], axis=0)
        away.append(swap(piece, "xl"))
    own = half(kernel, core, 1)
    other = swap(half(kernel, 1 - core, 1), "core")
    place = core * 2 + xl
    fits = [
        lax.dynamic_slice_in_dim(fit, jnp.bitwise_xor(place, k) * 512, 512, 0) for k in range(4)
    ]
    fits = lax.optimization_barrier(fits)

    weighted = weigh(core, both, partner, near, away, own, other)

    partial = lax.dot_general(
        weighted, blocks, (((0,), (1,)), ((), ())), preferred_element_type=F32
    )
    arrived = swap(half(partial, 1 - xl, 0).astype(BF), "xl")
    two = (half(partial, xl, 0) + arrived.astype(F32)).astype(BF)
    terms = lax.all_to_all(two.reshape(8, 64, 512), Z, 0, 0, tiled=False)
    low = total(terms).astype(BF)
    p0 = gather(low, Z, 8).reshape(512, 512)
    p1 = swap(p0, "xl")
    p2 = swap(p0, "core")
    p3 = swap(p1, "core")
    result = dot(p0, fits[0])
    result = result + dot(p2, fits[2])
    result = result + dot(p1, fits[1])
    result = result + dot(p3, fits[3])
    terms = lax.all_to_all((-result).astype(BF).reshape(8, 64, 2048), ("y", "xh"), 0, 0, tiled=False)
    return total(terms).astype(BF)


def solution(mesh):
    fine = Mesh(mesh.devices.reshape(tuple(size for _, size in SIZES)), NAMES)
    row, col = ROW, ("xl",) + Z + ("core",)
    return jax.shard_map(
        program,
        mesh=fine,
        in_specs=(P(row, col), P(col, row), P(col, row), P(row, col)),
        out_specs=P(row, col),
        check_vma=False,
    )
```

```python
import jax
import jax.numpy as jnp
from jax import lax
from jax.experimental import pallas as pl
from jax.experimental.pallas import tpu as pltpu
from jax.sharding import Mesh
from jax.sharding import PartitionSpec as P


BF = jnp.bfloat16
F32 = jnp.float32
ROW = ("xh", "y")
Z = ("zh", "zl")
SIZES = (("xh", 2), ("y", 4), ("xl", 2), ("zh", 4), ("zl", 2), ("core", 2))
NAMES = tuple(name for name, _ in SIZES)
PAIR = ((0, 1), (1, 0))
MATE = tuple((z, z ^ 1) for z in range(8))
STEPS = (0, 3, 1, 2)
ORDER = (1, 0, 7, 6, 3, 2, 5, 4)
OUTER = tuple((z, (z - 1) % 8 if z % 2 == 0 else (z + 1) % 8) for z in range(8))


def flat(coords):
    index = 0
    for (_, size), value in zip(SIZES, coords):
        index = index * size + value
    return index


def nu_pairs(flip):
    pairs = []
    for xh in range(2):
        for y in range(4):
            for xl in range(2):
                for zh in range(4):
                    for zl in range(2):
                        for core in range(2):
                            away = STEPS[y] if zl == 0 else -STEPS[y]
                            source = (xl, zh, xl ^ xh ^ flip, (zh + away) % 4, zl, core)
                            pairs.append((flat(source), flat((xh, y, xl, zh, zl, core))))
    return pairs


def dot(a, b):
    return lax.dot_general(a, b, (((0,), (0,)), ((), ())), preferred_element_type=F32)


def swap(x, axis):
    return lax.ppermute(x, axis, PAIR)


def gather(x, axes, count):
    copies = jnp.broadcast_to(x[None], (count,) + x.shape)
    return lax.all_to_all(copies, axes, 0, 0, tiled=False)


def ring(x):
    near, far = [x], [x]
    for step in range(1, 5):
        near.append(lax.ppermute(far[step - 1], Z, MATE))
        if step < 4:
            far.append(lax.ppermute(near[step - 1], Z, OUTER))
    return near + far[:0:-1]


def half(x, index, axis):
    size = x.shape[axis] // 2
    return lax.dynamic_slice_in_dim(x, index * size, size, axis)


def total(terms):
    parts = [terms[k].astype(F32) for k in range(terms.shape[0])]
    while len(parts) > 1:
        parts = [a + b for a, b in zip(parts[::2], parts[1::2])]
    return parts[0]


def ordered(index, own, other):
    first = jnp.where(index == 0, own, other)
    second = jnp.where(index == 0, other, own)
    return first, second


def weigh(places, nu_a, nu_b, near, away, own, other):
    def body(place_ref, nu_a_ref, nu_b_ref, *refs):
        near_refs, away_refs = refs[:8], refs[8:13]
        own_ref, other_ref, out_ref, mu_a, mu_b = refs[13:]
        across = {
            0: (away_refs[0], 0),
            1: (away_refs[1], 0),
            7: (away_refs[1], 64),
            2: (away_refs[2], 0),
            6: (away_refs[2], 64),
            3: (away_refs[3], 0),
            5: (away_refs[3], 64),
            4: (away_refs[4], 0),
        }
        sides = (place_ref[1], 1 - place_ref[1])
        for y in range(4):
            for o in range(2):
                n = ORDER[y * 2 + o]
                for x, (ref, start) in enumerate(((near_refs[n], 0), across[n])):
                    row = pl.multiple_of((y * 2 + sides[x]) * 64 + o * 32, 32)
                    mu_a[pl.ds(row, 32), :] = ref[start : start + 32, :]
                    mu_b[pl.ds(row, 32), :] = ref[start + 32 : start + 64, :]

        mine = place_ref[0]

        def tile(t, carry):
            start = pl.multiple_of(t * 256, 256)
            part_a = nu_a_ref[:, :, :, pl.ds(start, 256)].reshape(512, 256)
            part_b = nu_b_ref[:, :, :, pl.ds(start, 256)].reshape(512, 256)
            density = dot(part_a, mu_a[...]) + dot(part_b, mu_b[...])
            row = pl.multiple_of((t % 2) * 256, 256)
            ours = own_ref[pl.ds(row, 256), :]
            theirs = other_ref[pl.ds(row, 256), :]
            factor = jnp.where(t // 2 == mine, ours.astype(F32), theirs.astype(F32))
            out_ref[pl.ds(start, 256), :] = (density * factor).astype(BF)
            return carry

        lax.fori_loop(0, 4, tile, 0)

    vmem = pl.BlockSpec(memory_space=pltpu.VMEM)
    return pl.pallas_call(
        body,
        out_shape=jax.ShapeDtypeStruct((1024, 1024), BF),
        in_specs=[pl.BlockSpec(memory_space=pltpu.SMEM)] + [vmem] * 17,
        out_specs=vmem,
        scratch_shapes=[pltpu.VMEM((512, 1024), BF), pltpu.VMEM((512, 1024), BF)],
        compiler_params=pltpu.CompilerParams(vmem_limit_bytes=32 << 20),
        cost_estimate=pl.CostEstimate(
            flops=2 * 1024**3, bytes_accessed=10 << 20, transcendentals=0
        ),
    )(places, nu_a, nu_b, *near, *away, own, other)


def program(orbitals, kernel, applied, fit):
    core = lax.axis_index("core")
    xl = lax.axis_index("xl")
    zl = lax.axis_index("zl")

    bands = orbitals.T
    cross = swap(half(bands, 1 - zl, 1), "zl")
    piece = jnp.concatenate([cross, half(bands, zl, 1)], axis=0)
    arrivals = []
    for k in range(2):
        arrivals.append(lax.ppermute(piece, NAMES, nu_pairs(k)))
    both = gather(jnp.stack(arrivals), "y", 4)
    partner = swap(both, "core")
    own = gather(applied.T, ROW, 8)
    other = swap(own, "core")
    blocks = jnp.concatenate(ordered(core, own, other), axis=2).reshape(512, 1024)
    mu_own = half(bands, core, 1)
    mu_other = swap(half(bands, 1 - core, 1), "core")
    near = ring(jnp.concatenate([mu_own, mu_other], axis=0))
    away = []
    for a, b in ((0, 0), (1, 7), (2, 6), (3, 5), (4, 4)):
        piece = near[a] if a == b else jnp.concatenate([near[a], near[b]], axis=0)
        away.append(swap(piece, "xl"))
    own = half(kernel, core, 1)
    other = swap(half(kernel, 1 - core, 1), "core")
    place = core * 2 + xl
    fits = [
        lax.dynamic_slice_in_dim(fit, jnp.bitwise_xor(place, k) * 512, 512, 0) for k in range(4)
    ]
    fits = lax.optimization_barrier(fits)

    places = jnp.stack([core, lax.axis_index("xh")])
    weighted = weigh(places, both, partner, near, away, own, other)

    partial = lax.dot_general(
        weighted, blocks, (((0,), (1,)), ((), ())), preferred_element_type=F32
    )
    arrived = swap(half(partial, 1 - xl, 0).astype(BF), "xl")
    two = (half(partial, xl, 0) + arrived.astype(F32)).astype(BF)
    terms = lax.all_to_all(two.reshape(8, 64, 512), Z, 0, 0, tiled=False)
    low = total(terms).astype(BF)
    p0 = gather(low, Z, 8).reshape(512, 512)
    p1 = swap(p0, "xl")
    p2 = swap(p0, "core")
    result = dot(p0, fits[0])
    result = result + dot(p2, fits[2])
    p1, result = lax.optimization_barrier((p1, result))
    p3 = swap(p1, "core")
    result = result + dot(p1, fits[1])
    result = result + dot(p3, fits[3])
    terms = lax.all_to_all((-result).astype(BF).reshape(8, 64, 2048), ROW, 0, 0, tiled=False)
    return total(terms).astype(BF)


def solution(mesh):
    fine = Mesh(mesh.devices.reshape(tuple(size for _, size in SIZES)), NAMES)
    row, col = ROW, ("xl",) + Z + ("core",)
    return jax.shard_map(
        program,
        mesh=fine,
        in_specs=(P(row, col), P(col, row), P(col, row), P(row, col)),
        out_specs=P(row, col),
        check_vma=False,
    )
```

```python
import jax
import jax.numpy as jnp
from jax import lax
from jax.experimental import pallas as pl
from jax.experimental.pallas import tpu as pltpu
from jax.sharding import Mesh
from jax.sharding import PartitionSpec as P


BF = jnp.bfloat16
F32 = jnp.float32
ROW = ("xh", "y")
Z = ("zh", "zl")
SIZES = (("xh", 2), ("y", 4), ("xl", 2), ("zh", 4), ("zl", 2), ("core", 2))
NAMES = tuple(name for name, _ in SIZES)
PAIR = ((0, 1), (1, 0))
MATE = tuple((z, z ^ 1) for z in range(8))
OUTER = tuple((z, (z - 1) % 8 if z % 2 == 0 else (z + 1) % 8) for z in range(8))


def flat(coords):
    index = 0
    for (_, size), value in zip(SIZES, coords):
        index = index * size + value
    return index


def far_pairs():
    pairs = []
    for xh in range(2):
        for y in range(4):
            for xl in range(2):
                for zh in range(4):
                    for zl in range(2):
                        for core in range(2):
                            source = flat((xh, y, xl, zh, zl, core))
                            place = (2 * y + 2 - zh) % 4
                            pairs.append((source, flat((xl, place, xh, y, zl, core))))
    return pairs


def dot(a, b):
    return lax.dot_general(a, b, (((0,), (0,)), ((), ())), preferred_element_type=F32)


def swap(x, axis):
    return lax.ppermute(x, axis, PAIR)


def gather(x, axes, count):
    copies = jnp.broadcast_to(x[None], (count,) + x.shape)
    return lax.all_to_all(copies, axes, 0, 0, tiled=False)


def ring(x):
    near, far = [x], [x]
    for step in range(1, 5):
        near.append(lax.ppermute(far[step - 1], Z, MATE))
        if step < 4:
            far.append(lax.ppermute(near[step - 1], Z, OUTER))
    return near + far[:0:-1]


def half(x, index, axis):
    size = x.shape[axis] // 2
    return lax.dynamic_slice_in_dim(x, index * size, size, axis)


def total(terms):
    parts = [terms[k].astype(F32) for k in range(terms.shape[0])]
    while len(parts) > 1:
        parts = [a + b for a, b in zip(parts[::2], parts[1::2])]
    return parts[0]


def fan(ours, pair, over, both, applied):
    def body(ours_ref, pair_ref, over_ref, both_ref, applied_ref, out_ref):
        for k in range(4):
            out_ref[k, 0, 0, :, :1024] = ours_ref[...]
            out_ref[k, 0, 0, :, 1024:] = applied_ref[:32, :]
            out_ref[k, 0, 1, :, :1024] = pair_ref[...]
            out_ref[k, 0, 1, :, 1024:] = applied_ref[32:, :]
            out_ref[k, 1, 0] = over_ref[:, :1536]
            out_ref[k, 1, 1, :, :1024] = both_ref[...]
            out_ref[k, 1, 1, :, 1024:] = over_ref[:, 1536:]

    vmem = pl.BlockSpec(memory_space=pltpu.VMEM)
    return pl.pallas_call(
        body,
        out_shape=jax.ShapeDtypeStruct((4, 2, 2, 32, 1536), BF),
        in_specs=[vmem] * 5,
        out_specs=vmem,
        cost_estimate=pl.CostEstimate(flops=0, bytes_accessed=2 << 20, transcendentals=0),
    )(ours, pair, over, both, applied)


def weigh(places, nu_a, nu_b, near, away, own, other):
    def body(place_ref, nu_a_ref, nu_b_ref, *refs):
        near_refs, away_refs = refs[:8], refs[8:13]
        own_ref, other_ref, out_ref, mu_a, mu_b = refs[13:]
        across = {
            0: (away_refs[0], 0),
            1: (away_refs[1], 0),
            7: (away_refs[1], 64),
            2: (away_refs[2], 0),
            6: (away_refs[2], 64),
            3: (away_refs[3], 0),
            5: (away_refs[3], 64),
            4: (away_refs[4], 0),
        }
        for n in range(8):
            y = jnp.bitwise_and(place_ref[2] - place_ref[3] * (n // 2), 3)
            for x, (ref, start) in enumerate(((near_refs[n], 0), across[n])):
                side = place_ref[1] if x == 0 else 1 - place_ref[1]
                row = pl.multiple_of(((y * 2 + side) * 2 + n % 2) * 32, 32)
                mu_a[pl.ds(row, 32), :] = ref[start : start + 32, :]
                mu_b[pl.ds(row, 32), :] = ref[start + 32 : start + 64, :]

        mine = place_ref[0]

        def tile(t, carry):
            start = pl.multiple_of(t * 256, 256)
            part_a = nu_a_ref[:, :, :, :, pl.ds(start, 256)].reshape(512, 256)
            part_b = nu_b_ref[:, :, :, :, pl.ds(start, 256)].reshape(512, 256)
            density = dot(part_a, mu_a[...]) + dot(part_b, mu_b[...])
            row = pl.multiple_of((t % 2) * 256, 256)
            ours = own_ref[pl.ds(row, 256), :]
            theirs = other_ref[pl.ds(row, 256), :]
            factor = jnp.where(t // 2 == mine, ours.astype(F32), theirs.astype(F32))
            out_ref[pl.ds(start, 256), :] = (density * factor).astype(BF)
            return carry

        lax.fori_loop(0, 4, tile, 0)

    vmem = pl.BlockSpec(memory_space=pltpu.VMEM)
    return pl.pallas_call(
        body,
        out_shape=jax.ShapeDtypeStruct((1024, 1024), BF),
        in_specs=[pl.BlockSpec(memory_space=pltpu.SMEM)] + [vmem] * 17,
        out_specs=vmem,
        scratch_shapes=[pltpu.VMEM((512, 1024), BF), pltpu.VMEM((512, 1024), BF)],
        compiler_params=pltpu.CompilerParams(vmem_limit_bytes=32 << 20),
        cost_estimate=pl.CostEstimate(
            flops=2 * 1024**3, bytes_accessed=10 << 20, transcendentals=0
        ),
    )(places, nu_a, nu_b, *near, *away, own, other)


def program(orbitals, kernel, applied, fit):
    core = lax.axis_index("core")
    xl = lax.axis_index("xl")
    zl = lax.axis_index("zl")
    xh = lax.axis_index("xh")
    zh = lax.axis_index("zh")

    bands = orbitals.T
    rows = lax.ppermute(bands, NAMES, far_pairs())
    ours, theirs = half(rows, zl, 1), half(rows, 1 - zl, 1)
    left, right = applied.T[:32], applied.T[32:]
    pair = swap(theirs, "zl")
    over = swap(jnp.concatenate([ours, left, right], axis=1), "xh")
    both = lax.ppermute(theirs, ("xh", "zl"), ((0, 3), (1, 2), (2, 1), (3, 0)))
    copies = fan(ours, pair, over, both, applied.T)
    nu = lax.all_to_all(copies, "y", 0, 0, tiled=False)
    nu_partner = swap(nu, "core")

    def pick(c, k):
        sides = [v[:, :, :, :, 1024:].reshape(4, 2, 64, 512) for v in (nu, nu_partner)]
        mine, other = [jnp.where(xh == 0, v[:, k], v[:, 1 - k]) for v in sides]
        return jnp.where(core == c, mine, other)

    blocks = [jnp.concatenate([pick(0, k), pick(1, k)], axis=2) for k in range(2)]
    blocks = jnp.stack(blocks, axis=1).reshape(512, 1024)
    mu_own = half(bands, core, 1)
    mu_other = swap(half(bands, 1 - core, 1), "core")
    near = ring(jnp.concatenate([mu_own, mu_other], axis=0))
    away = []
    for a, b in ((0, 0), (1, 7), (2, 6), (3, 5), (4, 4)):
        piece = near[a] if a == b else jnp.concatenate([near[a], near[b]], axis=0)
        away.append(swap(piece, "xl"))
    own = half(kernel, core, 1)
    other = swap(half(kernel, 1 - core, 1), "core")
    place = core * 2 + xl
    fits = [
        lax.dynamic_slice_in_dim(fit, jnp.bitwise_xor(place, k) * 512, 512, 0) for k in range(4)
    ]
    fits = lax.optimization_barrier(fits)

    places = jnp.stack([core, jnp.bitwise_xor(xl, xh), zh + 2, 1 - 2 * zl])
    weighted = weigh(places, nu, nu_partner, near, away, own, other)

    partial = lax.dot_general(
        weighted, blocks, (((0,), (1,)), ((), ())), preferred_element_type=F32
    )
    arrived = swap(half(partial, 1 - xl, 0).astype(BF), "xl")
    two = (half(partial, xl, 0) + arrived.astype(F32)).astype(BF)
    terms = lax.all_to_all(two.reshape(8, 64, 512), Z, 0, 0, tiled=False)
    low = total(terms).astype(BF)
    p0 = gather(low, Z, 8).reshape(512, 512)
    p1 = swap(p0, "xl")
    p2 = swap(p0, "core")
    p3 = swap(p1, "core")
    result = dot(p0, fits[0])
    result = result + dot(p2, fits[2])
    result = result + dot(p1, fits[1])
    result = result + dot(p3, fits[3])
    terms = lax.all_to_all((-result).astype(BF).reshape(8, 64, 2048), ("y", "xh"), 0, 0, tiled=False)
    return total(terms).astype(BF)


def solution(mesh):
    fine = Mesh(mesh.devices.reshape(tuple(size for _, size in SIZES)), NAMES)
    row, col = ROW, ("xl",) + Z + ("core",)
    return jax.shard_map(
        program,
        mesh=fine,
        in_specs=(P(row, col), P(col, row), P(col, row), P(row, col)),
        out_specs=P(row, col),
        check_vma=False,
    )
```

```python
import jax
import jax.numpy as jnp
from jax import lax
from jax.experimental import pallas as pl
from jax.experimental.pallas import tpu as pltpu
from jax.sharding import Mesh
from jax.sharding import PartitionSpec as P


BF = jnp.bfloat16
F32 = jnp.float32
ROW = ("xh", "y")
Z = ("zh", "zl")
SIZES = (("xh", 2), ("y", 4), ("xl", 2), ("zh", 4), ("zl", 2), ("core", 2))
NAMES = tuple(name for name, _ in SIZES)
PAIR = ((0, 1), (1, 0))
MATE = tuple((z, z ^ 1) for z in range(8))
OUTER = tuple((z, (z - 1) % 8 if z % 2 == 0 else (z + 1) % 8) for z in range(8))


def flat(coords):
    index = 0
    for (_, size), value in zip(SIZES, coords):
        index = index * size + value
    return index


def far_pairs():
    pairs = []
    for xh in range(2):
        for y in range(4):
            for xl in range(2):
                for zh in range(4):
                    for zl in range(2):
                        for core in range(2):
                            source = flat((xh, y, xl, zh, zl, core))
                            place = (2 * y + 2 - zh) % 4
                            pairs.append((source, flat((xl, place, xh, y, zl, core))))
    return pairs


def dot(a, b):
    return lax.dot_general(a, b, (((0,), (0,)), ((), ())), preferred_element_type=F32)


def swap(x, axis):
    return lax.ppermute(x, axis, PAIR)


def ring(x):
    near, far = [x], [x]
    for step in range(1, 5):
        near.append(lax.ppermute(far[step - 1], Z, MATE))
        if step < 4:
            far.append(lax.ppermute(near[step - 1], Z, OUTER))
    return near + far[:0:-1]


def half(x, index, axis):
    size = x.shape[axis] // 2
    return lax.dynamic_slice_in_dim(x, index * size, size, axis)


def total(terms):
    parts = [terms[k].astype(F32) for k in range(terms.shape[0])]
    while len(parts) > 1:
        parts = [a + b for a, b in zip(parts[::2], parts[1::2])]
    return parts[0]


def fan(ours, pair, over, both, applied):
    def body(ours_ref, pair_ref, over_ref, both_ref, applied_ref, out_ref):
        for k in range(4):
            out_ref[k, 0, 0, :, :1024] = ours_ref[...]
            out_ref[k, 0, 0, :, 1024:] = applied_ref[:32, :]
            out_ref[k, 0, 1, :, :1024] = pair_ref[...]
            out_ref[k, 0, 1, :, 1024:] = applied_ref[32:, :]
            out_ref[k, 1, 0] = over_ref[:, :1536]
            out_ref[k, 1, 1, :, :1024] = both_ref[...]
            out_ref[k, 1, 1, :, 1024:] = over_ref[:, 1536:]

    vmem = pl.BlockSpec(memory_space=pltpu.VMEM)
    return pl.pallas_call(
        body,
        out_shape=jax.ShapeDtypeStruct((4, 2, 2, 32, 1536), BF),
        in_specs=[vmem] * 5,
        out_specs=vmem,
        cost_estimate=pl.CostEstimate(flops=0, bytes_accessed=2 << 20, transcendentals=0),
    )(ours, pair, over, both, applied)


def round_and_fan(terms):
    def body(terms_ref, out_ref):
        value = total(terms_ref[...]).astype(BF)
        for k in range(8):
            out_ref[k] = value

    vmem = pl.BlockSpec(memory_space=pltpu.VMEM)
    return pl.pallas_call(
        body,
        out_shape=jax.ShapeDtypeStruct(terms.shape, BF),
        in_specs=[vmem],
        out_specs=vmem,
        cost_estimate=pl.CostEstimate(flops=1 << 18, bytes_accessed=1 << 20, transcendentals=0),
    )(terms)


def weigh(places, nu_a, nu_b, near, away, own, other, first):
    def body(place_ref, nu_a_ref, nu_b_ref, *refs):
        near_refs, away_refs = refs[:8], refs[8:13]
        own_ref, other_ref, out_ref = refs[13:16]
        mu_a, mu_b = refs[-2:]
        points = pl.ds(pl.multiple_of(place_ref[4] * 512, 512), 512)
        across = {
            0: (away_refs[0], 0),
            1: (away_refs[1], 0),
            7: (away_refs[1], 64),
            2: (away_refs[2], 0),
            6: (away_refs[2], 64),
            3: (away_refs[3], 0),
            5: (away_refs[3], 64),
            4: (away_refs[4], 0),
        }
        for n in range(8):
            y = jnp.bitwise_and(place_ref[2] - place_ref[3] * (n // 2), 3)
            for x, (ref, start) in enumerate(((near_refs[n], 0), across[n])):
                side = place_ref[1] if x == 0 else 1 - place_ref[1]
                row = pl.multiple_of(((y * 2 + side) * 2 + n % 2) * 32, 32)
                mu_a[pl.ds(row, 32), :] = ref[start : start + 32, points]
                mu_b[pl.ds(row, 32), :] = ref[start + 32 : start + 64, points]

        mine = place_ref[0]

        def tile(t, carry):
            start = pl.multiple_of(t * 256, 256)
            part_a = nu_a_ref[:, :, :, :, pl.ds(start, 256)].reshape(512, 256)
            part_b = nu_b_ref[:, :, :, :, pl.ds(start, 256)].reshape(512, 256)
            density = dot(part_a, mu_a[...]) + dot(part_b, mu_b[...])
            row = pl.multiple_of((t % 2) * 256, 256)
            ours = own_ref[pl.ds(row, 256), points]
            theirs = other_ref[pl.ds(row, 256), points]
            factor = jnp.where(t // 2 == mine, ours.astype(F32), theirs.astype(F32))
            out_ref[pl.ds(start, 256), :] = (density * factor).astype(BF)
            return carry

        lax.fori_loop(0, 4, tile, 0)
        if first:
            flip = jnp.bitwise_xor(mine, 1)
            for ref, side in ((nu_a_ref, mine), (nu_b_ref, flip)):
                lanes = pl.ds(pl.multiple_of(side * 512, 512), 512)
                for y in range(4):
                    for k in range(2):
                        row = pl.multiple_of((y * 2 + jnp.bitwise_xor(place_ref[5], k)) * 64, 64)
                        values = ref[y, k, :, :, 1024:].reshape(64, 512)
                        refs[16][pl.ds(row, 64), lanes] = values

    vmem = pl.BlockSpec(memory_space=pltpu.VMEM)
    return pl.pallas_call(
        body,
        out_shape=[
            jax.ShapeDtypeStruct((1024, 512), BF),
            jax.ShapeDtypeStruct((512, 1024), BF),
        ][: 1 + first],
        in_specs=[pl.BlockSpec(memory_space=pltpu.SMEM)] + [vmem] * 17,
        out_specs=[vmem] * (1 + first),
        scratch_shapes=[pltpu.VMEM((512, 512), BF), pltpu.VMEM((512, 512), BF)],
        compiler_params=pltpu.CompilerParams(vmem_limit_bytes=32 << 20),
        cost_estimate=pl.CostEstimate(
            flops=1024**3, bytes_accessed=10 << 20, transcendentals=0
        ),
    )(places, nu_a, nu_b, *near, *away, own, other)


def program(orbitals, kernel, applied, fit):
    core = lax.axis_index("core")
    xl = lax.axis_index("xl")
    zl = lax.axis_index("zl")
    xh = lax.axis_index("xh")
    zh = lax.axis_index("zh")

    bands = orbitals.T
    rows = lax.ppermute(bands, NAMES, far_pairs())
    ours, theirs = half(rows, zl, 1), half(rows, 1 - zl, 1)
    left, right = applied.T[:32], applied.T[32:]
    pair = swap(theirs, "zl")
    over = swap(jnp.concatenate([ours, left, right], axis=1), "xh")
    both = lax.ppermute(theirs, ("xh", "zl"), ((0, 3), (1, 2), (2, 1), (3, 0)))
    copies = fan(ours, pair, over, both, applied.T)
    nu = lax.all_to_all(copies, "y", 0, 0, tiled=False)
    nu_partner = swap(nu, "core")
    mu_own = half(bands, core, 1)
    mu_other = swap(half(bands, 1 - core, 1), "core")
    near = ring(jnp.concatenate([mu_own, mu_other], axis=0))
    away = []
    for a, b in ((0, 0), (1, 7), (2, 6), (3, 5), (4, 4)):
        piece = near[a] if a == b else jnp.concatenate([near[a], near[b]], axis=0)
        away.append(swap(piece, "xl"))
    own = half(kernel, core, 1)
    other = swap(half(kernel, 1 - core, 1), "core")
    place = core * 2 + xl
    fits = [
        lax.dynamic_slice_in_dim(fit, jnp.bitwise_xor(place, k) * 512, 512, 0) for k in range(4)
    ]
    fits = lax.optimization_barrier(fits)

    operands = (nu, nu_partner, near, away, own, other)
    shared = [core, jnp.bitwise_xor(xl, xh), zh + 2, 1 - 2 * zl]
    far_half, blocks = weigh(jnp.stack(shared + [1 - xl, xh]), *operands, True)
    (own_half,) = weigh(jnp.stack(shared + [xl, xh]), *operands, False)

    def project(weighted):
        return lax.dot_general(
            weighted, blocks, (((0,), (1,)), ((), ())), preferred_element_type=F32
        )

    arrived = swap(project(far_half).astype(BF), "xl")
    two = (project(own_half) + arrived.astype(F32)).astype(BF)
    terms = lax.all_to_all(two.reshape(8, 64, 512), Z, 0, 0, tiled=False)
    p0 = lax.all_to_all(round_and_fan(terms), Z, 0, 0, tiled=False).reshape(512, 512)
    p1 = swap(p0, "xl")
    p2 = swap(p0, "core")
    result = dot(p0, fits[0])
    result = result + dot(p2, fits[2])
    p1, result = lax.optimization_barrier((p1, result))
    p3 = swap(p1, "core")
    result = result + dot(p1, fits[1])
    result = result + dot(p3, fits[3])
    terms = lax.all_to_all(
        (-result).astype(BF).reshape(8, 64, 2048), ("y", "xh"), 0, 0, tiled=False
    )
    return total(terms).astype(BF)


def solution(mesh):
    fine = Mesh(mesh.devices.reshape(tuple(size for _, size in SIZES)), NAMES)
    row, col = ROW, ("xl",) + Z + ("core",)
    return jax.shard_map(
        program,
        mesh=fine,
        in_specs=(P(row, col), P(col, row), P(col, row), P(row, col)),
        out_specs=P(row, col),
        check_vma=False,
    )
```

```python
import jax
import jax.numpy as jnp
from jax import lax
from jax.experimental import pallas as pl
from jax.experimental.pallas import tpu as pltpu
from jax.sharding import Mesh
from jax.sharding import PartitionSpec as P


BF = jnp.bfloat16
F32 = jnp.float32
ROW = ("xh", "y")
Z = ("zh", "zl")
SIZES = (("xh", 2), ("y", 4), ("xl", 2), ("zh", 4), ("zl", 2), ("core", 2))
NAMES = tuple(name for name, _ in SIZES)
PAIR = ((0, 1), (1, 0))
MATE = tuple((z, z ^ 1) for z in range(8))
OUTER = tuple((z, (z - 1) % 8 if z % 2 == 0 else (z + 1) % 8) for z in range(8))


def flat(coords):
    index = 0
    for (_, size), value in zip(SIZES, coords):
        index = index * size + value
    return index


def far_pairs():
    pairs = []
    for xh in range(2):
        for y in range(4):
            for xl in range(2):
                for zh in range(4):
                    for zl in range(2):
                        for core in range(2):
                            source = flat((xh, y, xl, zh, zl, core))
                            place = (2 * y + 2 - zh) % 4
                            pairs.append((source, flat((xl, place, xh, y, zl, core))))
    return pairs


def dot(a, b):
    return lax.dot_general(a, b, (((0,), (0,)), ((), ())), preferred_element_type=F32)


def swap(x, axis):
    return lax.ppermute(x, axis, PAIR)


def gather(x, axes, count):
    copies = jnp.broadcast_to(x[None], (count,) + x.shape)
    return lax.all_to_all(copies, axes, 0, 0, tiled=False)


def ring(x):
    near, far = [x], [x]
    for step in range(1, 5):
        near.append(lax.ppermute(far[step - 1], Z, MATE))
        if step < 4:
            far.append(lax.ppermute(near[step - 1], Z, OUTER))
    return near + far[:0:-1]


def half(x, index, axis):
    size = x.shape[axis] // 2
    return lax.dynamic_slice_in_dim(x, index * size, size, axis)


def total(terms):
    parts = [terms[k].astype(F32) for k in range(terms.shape[0])]
    while len(parts) > 1:
        parts = [a + b for a, b in zip(parts[::2], parts[1::2])]
    return parts[0]


def fan(ours, pair, over, both, applied):
    def body(ours_ref, pair_ref, over_ref, both_ref, applied_ref, out_ref):
        for k in range(4):
            out_ref[k, 0, 0, :, :1024] = ours_ref[...]
            out_ref[k, 0, 0, :, 1024:] = applied_ref[:32, :]
            out_ref[k, 0, 1, :, :1024] = pair_ref[...]
            out_ref[k, 0, 1, :, 1024:] = applied_ref[32:, :]
            out_ref[k, 1, 0] = over_ref[:, :1536]
            out_ref[k, 1, 1, :, :1024] = both_ref[...]
            out_ref[k, 1, 1, :, 1024:] = over_ref[:, 1536:]

    vmem = pl.BlockSpec(memory_space=pltpu.VMEM)
    return pl.pallas_call(
        body,
        out_shape=jax.ShapeDtypeStruct((4, 2, 2, 32, 1536), BF),
        in_specs=[vmem] * 5,
        out_specs=vmem,
        cost_estimate=pl.CostEstimate(flops=0, bytes_accessed=2 << 20, transcendentals=0),
    )(ours, pair, over, both, applied)


def weigh(places, nu_a, nu_b, near, away, own, other, first):
    def body(place_ref, nu_a_ref, nu_b_ref, *refs):
        near_refs, away_refs = refs[:8], refs[8:13]
        own_ref, other_ref, out_ref = refs[13:16]
        mu_a, mu_b = refs[-2:]
        points = pl.ds(pl.multiple_of(place_ref[4] * 512, 512), 512)
        across = {
            0: (away_refs[0], 0),
            1: (away_refs[1], 0),
            7: (away_refs[1], 64),
            2: (away_refs[2], 0),
            6: (away_refs[2], 64),
            3: (away_refs[3], 0),
            5: (away_refs[3], 64),
            4: (away_refs[4], 0),
        }
        for n in range(8):
            y = jnp.bitwise_and(place_ref[2] - place_ref[3] * (n // 2), 3)
            for x, (ref, start) in enumerate(((near_refs[n], 0), across[n])):
                side = place_ref[1] if x == 0 else 1 - place_ref[1]
                row = pl.multiple_of(((y * 2 + side) * 2 + n % 2) * 32, 32)
                mu_a[pl.ds(row, 32), :] = ref[start : start + 32, points]
                mu_b[pl.ds(row, 32), :] = ref[start + 32 : start + 64, points]

        mine = place_ref[0]

        def tile(t, carry):
            start = pl.multiple_of(t * 256, 256)
            part_a = nu_a_ref[:, :, :, :, pl.ds(start, 256)].reshape(512, 256)
            part_b = nu_b_ref[:, :, :, :, pl.ds(start, 256)].reshape(512, 256)
            density = dot(part_a, mu_a[...]) + dot(part_b, mu_b[...])
            row = pl.multiple_of((t % 2) * 256, 256)
            ours = own_ref[pl.ds(row, 256), points]
            theirs = other_ref[pl.ds(row, 256), points]
            factor = jnp.where(t // 2 == mine, ours.astype(F32), theirs.astype(F32))
            out_ref[pl.ds(start, 256), :] = (density * factor).astype(BF)
            return carry

        lax.fori_loop(0, 4, tile, 0)
        if first:
            flip = jnp.bitwise_xor(mine, 1)
            for ref, side in ((nu_a_ref, mine), (nu_b_ref, flip)):
                lanes = pl.ds(pl.multiple_of(side * 512, 512), 512)
                for y in range(4):
                    for k in range(2):
                        row = ((1 - k) * 4 + y) * 64
                        values = ref[y, k, :, :, 1024:].reshape(64, 512)
                        refs[16][row : row + 64, lanes] = values

    vmem = pl.BlockSpec(memory_space=pltpu.VMEM)
    return pl.pallas_call(
        body,
        out_shape=[
            jax.ShapeDtypeStruct((1024, 512), BF),
            jax.ShapeDtypeStruct((512, 1024), BF),
        ][: 1 + first],
        in_specs=[pl.BlockSpec(memory_space=pltpu.SMEM)] + [vmem] * 17,
        out_specs=[vmem] * (1 + first),
        scratch_shapes=[pltpu.VMEM((512, 512), BF), pltpu.VMEM((512, 512), BF)],
        compiler_params=pltpu.CompilerParams(vmem_limit_bytes=32 << 20),
        cost_estimate=pl.CostEstimate(
            flops=1024**3, bytes_accessed=10 << 20, transcendentals=0
        ),
    )(places, nu_a, nu_b, *near, *away, own, other)


def program(orbitals, kernel, applied, fit):
    core = lax.axis_index("core")
    xl = lax.axis_index("xl")
    zl = lax.axis_index("zl")
    xh = lax.axis_index("xh")
    zh = lax.axis_index("zh")

    bands = orbitals.T
    rows = lax.ppermute(bands, NAMES, far_pairs())
    ours, theirs = half(rows, zl, 1), half(rows, 1 - zl, 1)
    left, right = applied.T[:32], applied.T[32:]
    pair = swap(theirs, "zl")
    over = swap(jnp.concatenate([ours, left, right], axis=1), "xh")
    both = lax.ppermute(theirs, ("xh", "zl"), ((0, 3), (1, 2), (2, 1), (3, 0)))
    copies = fan(ours, pair, over, both, applied.T)
    nu = lax.all_to_all(copies, "y", 0, 0, tiled=False)
    nu_partner = swap(nu, "core")
    mu_own = half(bands, core, 1)
    mu_other = swap(half(bands, 1 - core, 1), "core")
    near = ring(jnp.concatenate([mu_own, mu_other], axis=0))
    away = []
    for a, b in ((0, 0), (1, 7), (2, 6), (3, 5), (4, 4)):
        piece = near[a] if a == b else jnp.concatenate([near[a], near[b]], axis=0)
        away.append(swap(piece, "xl"))
    own = half(kernel, core, 1)
    other = swap(half(kernel, 1 - core, 1), "core")
    place = core * 2 + xl
    fits = [
        lax.dynamic_slice_in_dim(fit, jnp.bitwise_xor(place, k) * 512, 512, 0) for k in range(4)
    ]
    fits = lax.optimization_barrier(fits)

    operands = (nu, nu_partner, near, away, own, other)
    shared = [core, jnp.bitwise_xor(xl, xh), zh + 2, 1 - 2 * zl]
    far_half, blocks = weigh(jnp.stack(shared + [1 - xl]), *operands, True)
    (own_half,) = weigh(jnp.stack(shared + [xl]), *operands, False)

    def project(weighted):
        return lax.dot_general(
            weighted, blocks, (((0,), (1,)), ((), ())), preferred_element_type=F32
        )

    arrived = swap(project(far_half).astype(BF), "xl")
    mine = lax.optimization_barrier(project(own_half))
    two = (mine + arrived.astype(F32)).astype(BF)
    terms = lax.all_to_all(two.reshape(8, 64, 512), Z, 0, 0, tiled=False)
    p0 = gather(total(terms).astype(BF), Z, 8).reshape(512, 512)
    p1 = swap(p0, "xl")
    p2 = swap(p0, "core")
    p3 = swap(p1, "core")
    sums = []
    for h in range(2):
        part = slice(h * 256, h * 256 + 256)
        result = dot(p0[:, part], fits[0])
        result = result + dot(p2[:, part], fits[2])
        result = result + dot(p1[:, part], fits[1])
        result = result + dot(p3[:, part], fits[3])
        terms = lax.all_to_all(
            (-result).astype(BF).reshape(4, 64, 2048), "y", 0, 0, tiled=False
        )
        sums.append(total(terms))
    crossed = swap(sums[0].astype(BF), "xh")
    return (sums[1] + crossed.astype(F32)).astype(BF)


def solution(mesh):
    fine = Mesh(mesh.devices.reshape(tuple(size for _, size in SIZES)), NAMES)
    row, col = ROW, ("xl",) + Z + ("core",)
    return jax.shard_map(
        program,
        mesh=fine,
        in_specs=(P(row, col), P(col, row), P(col, row), P(row, col)),
        out_specs=P(row, col),
        check_vma=False,
    )
```

```python
import jax
import jax.numpy as jnp
from jax import lax
from jax.experimental import pallas as pl
from jax.experimental.pallas import tpu as pltpu
from jax.sharding import Mesh
from jax.sharding import PartitionSpec as P


BF = jnp.bfloat16
F32 = jnp.float32
ROW = ("xh", "y")
Z = ("zh", "zl")
SIZES = (("xh", 2), ("y", 4), ("xl", 2), ("zh", 4), ("zl", 2), ("core", 2))
NAMES = tuple(name for name, _ in SIZES)
PAIR = ((0, 1), (1, 0))
MATE = tuple((z, z ^ 1) for z in range(8))
OUTER = tuple((z, (z - 1) % 8 if z % 2 == 0 else (z + 1) % 8) for z in range(8))


def flat(coords):
    index = 0
    for (_, size), value in zip(SIZES, coords):
        index = index * size + value
    return index


def far_pairs():
    pairs = []
    for xh in range(2):
        for y in range(4):
            for xl in range(2):
                for zh in range(4):
                    for zl in range(2):
                        for core in range(2):
                            source = flat((xh, y, xl, zh, zl, core))
                            place = (2 * y + 2 - zh) % 4
                            pairs.append((source, flat((xl, place, xh, y, zl, core))))
    return pairs


def dot(a, b):
    return lax.dot_general(a, b, (((0,), (0,)), ((), ())), preferred_element_type=F32)


def swap(x, axis):
    return lax.ppermute(x, axis, PAIR)


def gather(x, axes, count):
    copies = jnp.broadcast_to(x[None], (count,) + x.shape)
    return lax.all_to_all(copies, axes, 0, 0, tiled=False)


def ring(x):
    near, far = [x], [x]
    for step in range(1, 5):
        near.append(lax.ppermute(far[step - 1], Z, MATE))
        if step < 4:
            far.append(lax.ppermute(near[step - 1], Z, OUTER))
    return near + far[:0:-1]


def half(x, index, axis):
    size = x.shape[axis] // 2
    return lax.dynamic_slice_in_dim(x, index * size, size, axis)


def total(terms):
    parts = [terms[k].astype(F32) for k in range(terms.shape[0])]
    while len(parts) > 1:
        parts = [a + b for a, b in zip(parts[::2], parts[1::2])]
    return parts[0]


def fan(ours, pair, over, both, applied):
    def body(ours_ref, pair_ref, over_ref, both_ref, applied_ref, out_ref):
        for k in range(4):
            out_ref[k, 0, 0, :, :1024] = ours_ref[...]
            out_ref[k, 0, 0, :, 1024:] = applied_ref[:32, :]
            out_ref[k, 0, 1, :, :1024] = pair_ref[...]
            out_ref[k, 0, 1, :, 1024:] = applied_ref[32:, :]
            out_ref[k, 1, 0] = over_ref[:, :1536]
            out_ref[k, 1, 1, :, :1024] = both_ref[...]
            out_ref[k, 1, 1, :, 1024:] = over_ref[:, 1536:]

    vmem = pl.BlockSpec(memory_space=pltpu.VMEM)
    return pl.pallas_call(
        body,
        out_shape=jax.ShapeDtypeStruct((4, 2, 2, 32, 1536), BF),
        in_specs=[vmem] * 5,
        out_specs=vmem,
        cost_estimate=pl.CostEstimate(flops=0, bytes_accessed=2 << 20, transcendentals=0),
    )(ours, pair, over, both, applied)


def weigh(places, nu_a, nu_b, near, away, own, other, first):
    def body(place_ref, nu_a_ref, nu_b_ref, *refs):
        near_refs, away_refs = refs[:8], refs[8:13]
        own_ref, other_ref, out_ref = refs[13:16]
        mu_a, mu_b = refs[-2:]
        points = pl.ds(pl.multiple_of(place_ref[4] * 512, 512), 512)
        across = {
            0: (away_refs[0], 0),
            1: (away_refs[1], 0),
            7: (away_refs[1], 64),
            2: (away_refs[2], 0),
            6: (away_refs[2], 64),
            3: (away_refs[3], 0),
            5: (away_refs[3], 64),
            4: (away_refs[4], 0),
        }
        for n in range(8):
            y = jnp.bitwise_and(place_ref[2] - place_ref[3] * (n // 2), 3)
            for x, (ref, start) in enumerate(((near_refs[n], 0), across[n])):
                side = place_ref[1] if x == 0 else 1 - place_ref[1]
                row = pl.multiple_of(((y * 2 + side) * 2 + n % 2) * 32, 32)
                mu_a[pl.ds(row, 32), :] = ref[start : start + 32, points]
                mu_b[pl.ds(row, 32), :] = ref[start + 32 : start + 64, points]

        mine = place_ref[0]

        def tile(t, carry):
            start = pl.multiple_of(t * 256, 256)
            part_a = nu_a_ref[:, :, :, :, pl.ds(start, 256)].reshape(512, 256)
            part_b = nu_b_ref[:, :, :, :, pl.ds(start, 256)].reshape(512, 256)
            density = dot(part_a, mu_a[...]) + dot(part_b, mu_b[...])
            row = pl.multiple_of((t % 2) * 256, 256)
            ours = own_ref[pl.ds(row, 256), points]
            theirs = other_ref[pl.ds(row, 256), points]
            factor = jnp.where(t // 2 == mine, ours.astype(F32), theirs.astype(F32))
            out_ref[pl.ds(start, 256), :] = (density * factor).astype(BF)
            return carry

        lax.fori_loop(0, 4, tile, 0)
        if first:
            flip = jnp.bitwise_xor(mine, 1)
            for ref, side in ((nu_a_ref, mine), (nu_b_ref, flip)):
                lanes = pl.ds(pl.multiple_of(side * 512, 512), 512)
                for y in range(4):
                    for k in range(2):
                        row = pl.multiple_of((y * 2 + jnp.bitwise_xor(place_ref[5], k)) * 64, 64)
                        values = ref[y, k, :, :, 1024:].reshape(64, 512)
                        refs[16][pl.ds(row, 64), lanes] = values

    vmem = pl.BlockSpec(memory_space=pltpu.VMEM)
    return pl.pallas_call(
        body,
        out_shape=[
            jax.ShapeDtypeStruct((1024, 512), BF),
            jax.ShapeDtypeStruct((512, 1024), BF),
        ][: 1 + first],
        in_specs=[pl.BlockSpec(memory_space=pltpu.SMEM)] + [vmem] * 17,
        out_specs=[vmem] * (1 + first),
        scratch_shapes=[pltpu.VMEM((512, 512), BF), pltpu.VMEM((512, 512), BF)],
        compiler_params=pltpu.CompilerParams(vmem_limit_bytes=32 << 20),
        cost_estimate=pl.CostEstimate(
            flops=1024**3, bytes_accessed=10 << 20, transcendentals=0
        ),
    )(places, nu_a, nu_b, *near, *away, own, other)


def program(orbitals, kernel, applied, fit):
    core = lax.axis_index("core")
    xl = lax.axis_index("xl")
    zl = lax.axis_index("zl")
    xh = lax.axis_index("xh")
    zh = lax.axis_index("zh")

    bands = orbitals.T
    rows = lax.ppermute(bands, NAMES, far_pairs())
    ours, theirs = half(rows, zl, 1), half(rows, 1 - zl, 1)
    left, right = applied.T[:32], applied.T[32:]
    pair = swap(theirs, "zl")
    over = swap(jnp.concatenate([ours, left, right], axis=1), "xh")
    both = lax.ppermute(theirs, ("xh", "zl"), ((0, 3), (1, 2), (2, 1), (3, 0)))
    copies = fan(ours, pair, over, both, applied.T)
    nu = lax.all_to_all(copies, "y", 0, 0, tiled=False)
    nu_partner = swap(nu, "core")
    mu_own = half(bands, core, 1)
    mu_other = swap(half(bands, 1 - core, 1), "core")
    near = ring(jnp.concatenate([mu_own, mu_other], axis=0))
    away = []
    for a, b in ((0, 0), (1, 7), (2, 6), (3, 5), (4, 4)):
        piece = near[a] if a == b else jnp.concatenate([near[a], near[b]], axis=0)
        away.append(swap(piece, "xl"))
    own = half(kernel, core, 1)
    other = swap(half(kernel, 1 - core, 1), "core")
    place = core * 2 + xl
    fits = [
        lax.dynamic_slice_in_dim(fit, jnp.bitwise_xor(place, k) * 512, 512, 0) for k in range(4)
    ]
    fits = lax.optimization_barrier(fits)

    operands = (nu, nu_partner, near, away, own, other)
    shared = [core, jnp.bitwise_xor(xl, xh), zh + 2, 1 - 2 * zl]
    far_half, blocks = weigh(jnp.stack(shared + [1 - xl, xh]), *operands, True)
    (own_half,) = weigh(jnp.stack(shared + [xl, xh]), *operands, False)

    def project(weighted):
        return lax.dot_general(
            weighted, blocks, (((0,), (1,)), ((), ())), preferred_element_type=F32
        )

    arrived = swap(project(far_half).astype(BF), "xl")
    mine = lax.optimization_barrier(project(own_half))
    two = (mine + arrived.astype(F32)).astype(BF)
    terms = lax.all_to_all(two.reshape(8, 64, 512), Z, 0, 0, tiled=False)
    p0 = gather(total(terms).astype(BF), Z, 8).reshape(512, 512)
    p1 = swap(p0, "xl")
    p2 = swap(p0, "core")
    result = dot(p0, fits[0])
    result = result + dot(p2, fits[2])
    p1, result = lax.optimization_barrier((p1, result))
    p3 = swap(p1, "core")
    result = result + dot(p1, fits[1])
    result = result + dot(p3, fits[3])
    terms = lax.all_to_all(
        (-result).astype(BF).reshape(8, 64, 2048), ("y", "xh"), 0, 0, tiled=False
    )
    return total(terms).astype(BF)


def solution(mesh):
    fine = Mesh(mesh.devices.reshape(tuple(size for _, size in SIZES)), NAMES)
    row, col = ROW, ("xl",) + Z + ("core",)
    return jax.shard_map(
        program,
        mesh=fine,
        in_specs=(P(row, col), P(col, row), P(col, row), P(row, col)),
        out_specs=P(row, col),
        check_vma=False,
    )
```
